256 devices in a mesh: dp: 32 (over x_hi, z, core), tensor: 8 (over y, x_lo).
Axes of the slice: x: 4 (x_hi: 2, x_lo: 2; x = x_hi * 2 + x_lo), y: 4, z: 8, core: 2. Of those that a mesh axis runs over, the one named last changes fastest.
Arguments:
- tokens: bfloat16 [32768, 8192], P(('dp', 'tensor')), may hold values from -6 to 6
- out_grad: bfloat16 [32768, 26624], P('dp', 'tensor')
- delta: float32 [8, 128, 128, 128], P('tensor', 'dp'), may hold values from -3 to 3
- block_rows: int32 [1024], P('tensor'), may hold values from 0 to 63, as said below
- block_cols: int32 [1024], P('tensor'), may hold values from 0 to 25, as said below
- block_count: int32 [8], P('tensor'), may hold values from 1 to 128, as said below
Outputs:
- new_delta: float32 [8, 128, 128, 128], P('tensor', 'dp')
The draws below stay inside these ranges and needn't reach their ends.
Inputs may be any that keep to these rules, and one draw needn't show every extreme that they name: `block_rows`: entry t * 128 + k names the row block of slot k of tensor shard t; the slots of one shard name distinct pairs of row and column block. `block_cols`: entry t * 128 + k names the column block, counted within shard t's columns, of slot k of shard t. Slots 0 to block_count[t] - 1 of shard t are live, the rest are padding; some shard has all 128 live.
All inputs are finite; a program needn't handle non-finite values.
Results may differ from the reference program's by a relative error of at most 0.0003.
Values may be sent and summed in bfloat16 or wider, within the bound.
No kernel may reach another device: no remote copies, remote signals or barrier semaphores. Data moves between devices by JAX's collectives and lax.ppermute only.
A program may use at most 192 MiB of HBM per device.

```python
import math
import jax
import jax.numpy as jnp
from jax import lax

D = 8192
F = 26624
BLK = 128
KMAX = 128
GROUP = 32
TP_WAYS = 8
TOKENS = 32768
RB = 64
CB = 26


def index_table(key):
    shard_keys = jax.random.split(jax.random.fold_in(key, 7), TP_WAYS)
    chosen = jax.vmap(lambda one_key: jax.random.permutation(one_key, RB * CB)[:KMAX])(shard_keys)
    return chosen.astype(jnp.int32)


def draw_block_rows(key, part):
    return (index_table(key) // CB).reshape(-1).astype(jnp.int32)


def draw_block_cols(key, part):
    return (index_table(key) % CB).reshape(-1).astype(jnp.int32)


def draw_block_count(key, part):
    counts = jax.random.randint(jax.random.fold_in(key, 11), (TP_WAYS,), KMAX // 4, KMAX + 1)
    fullest = jax.random.randint(jax.random.fold_in(key, 13), (), 0, TP_WAYS)
    return jnp.where(jnp.arange(TP_WAYS, dtype=jnp.int32) == fullest, KMAX, counts).astype(jnp.int32)


def draw_out_grad(key, part):
    base_key, spread_key = jax.random.split(key, 2)
    position = jnp.arange(F, dtype=jnp.float32) / (F - 1)
    spread = jnp.exp(jax.random.uniform(spread_key, (F,)) * math.log(10.0))
    values = jax.random.truncated_normal(base_key, -4.0, 4.0, (TOKENS, F))
    ramp = 1.0 + 2.0 * position
    return (values * (ramp * spread)[None, :]).astype(jnp.bfloat16)


def steps_of(rng, dims, cuts, low, top_value):
    def one(dim, blocks):
        steps = jax.random.uniform(jax.random.fold_in(jax.random.fold_in(rng, 6), dim), (blocks,), jnp.float32, low / len(cuts), top_value / len(cuts))
        return jnp.repeat(jnp.exp(steps), dims[dim] // blocks).reshape((-1,) + (1,) * (len(dims) - dim - 1))

    factor_of = one(*cuts[0])
    for cut in cuts[1:]:
        factor_of = factor_of * one(*cut)
    return factor_of


def gaussian(rng, dims, scale, reach, pieces=(), held_as=jnp.bfloat16):
    entries = scale * jax.random.normal(rng, dims, jnp.float32)
    if pieces:
        entries = entries * steps_of(rng, dims, pieces, -0.22, 0.18)
    return jnp.clip(entries, -reach, reach).astype(held_as)


def setup_inputs(seed: int = 0) -> dict:
    key_of = jax.random.split(jax.random.key(seed), 7)
    tokens = gaussian(key_of[0], (TOKENS, D), 1.0, 6.0, ((0, 256),))
    out_grad = draw_out_grad(jax.random.fold_in(key_of[6], 71), 0)
    delta = gaussian(key_of[2], (TP_WAYS, KMAX, BLK, BLK), 0.5, 3.0, ((0, 8), (1, 32)), jnp.float32)
    block_rows = draw_block_rows(jax.random.fold_in(key_of[6], 71), 0)
    block_cols = draw_block_cols(jax.random.fold_in(key_of[6], 71), 0)
    block_count = draw_block_count(jax.random.fold_in(key_of[6], 71), 0)
    return {"tokens": tokens, "out_grad": out_grad, "delta": delta, "block_rows": block_rows, "block_cols": block_cols, "block_count": block_count}


def reference(tokens, out_grad, delta, block_rows, block_cols, block_count):
    token_tiles = tokens.reshape(TOKENS, D // BLK, BLK)
    grad_tiles = out_grad.reshape(TOKENS, F // BLK, BLK)
    per_shard = F // (TP_WAYS * BLK)
    groups_shard = KMAX // GROUP

    def one_group(group_index):
        row_ids = lax.dynamic_slice_in_dim(block_rows, group_index * GROUP, GROUP).astype(jnp.int32)
        shard_index = (group_index // groups_shard).astype(jnp.int32)
        col_ids = (lax.dynamic_slice_in_dim(block_cols, group_index * GROUP, GROUP) + shard_index * per_shard).astype(jnp.int32)
        token_cols = jnp.take(token_tiles, row_ids, axis=1).astype(jnp.float32)
        grad_cols = jnp.take(grad_tiles, col_ids, axis=1).astype(jnp.float32)
        return jnp.einsum('rkc,rkd->kcd', token_cols, grad_cols)
    block_grads = lax.map(one_group, jnp.arange(TP_WAYS * groups_shard, dtype=jnp.int32))
    block_grads = block_grads.reshape(TP_WAYS, KMAX, BLK, BLK)
    live_mask = (jnp.arange(KMAX, dtype=jnp.int32)[None, :] < block_count[:, None]).astype(jnp.float32)
    block_grads = block_grads * live_mask[:, :, None, None]
    square_sum = jnp.sum(block_grads * block_grads)
    norm_limit = BLK * math.sqrt(TP_WAYS * KMAX)
    factor = jnp.minimum(jnp.float32(1.0), norm_limit / jnp.sqrt(square_sum + 1e-06))
    return delta - 0.5 * factor * block_grads
```

```python
import functools
import math

import jax
import jax.numpy as jnp
from jax import lax
from jax.experimental import pallas as pl
from jax.experimental.pallas import tpu as pltpu
from jax.sharding import PartitionSpec as P


UNROLL = 8
XHI, ZN, CORES = 2, 8, 2
X_SWAP = [(t, t ^ 1) for t in range(8)]
Y_UP = [(t, (t + 2) % 8) for t in range(8)]
Y_DOWN = [(t, (t + 6) % 8) for t in range(8)]
CORE_SWAP = [(d, d ^ 1) for d in range(32)]
X_HI_SWAP = [(d, d ^ 16) for d in range(32)]
SAME_CORE = [[xh * 16 + z * 2 + c for xh in range(2) for z in range(8)] for c in range(2)]


def z_swap(bit):
    return [(d, d ^ (bit * 2)) for d in range(32)]


def grads_kernel(layout, first, meta, rows, cols, *refs):
    count = len(layout)
    pieces = refs[:count]
    grad_hbm = refs[count]
    rest = refs[count + 1 :]
    if first:
        out_hbm, x_buf, g_buf, o_buf, in_sem, out_sem = rest
    else:
        acc_hbm, send_hbm, keep_hbm, x_buf, g_buf, o_buf, in_sem, out_sem = rest
    slots = o_buf.shape[0]
    half = slots // 2
    copies = []
    at = 0
    for index, (source, start, size) in enumerate(layout):
        copies.append(
            pltpu.make_async_copy(pieces[index], x_buf.at[pl.ds(at, size), :], in_sem.at[2 * index])
        )
        row = pl.multiple_of(meta[source] * 128 + start, 32)
        copies.append(
            pltpu.make_async_copy(
                grad_hbm.at[pl.ds(row, size), :], g_buf.at[pl.ds(at, size), :], in_sem.at[2 * index + 1]
            )
        )
        at += size
    if not first:
        copies.append(pltpu.make_async_copy(acc_hbm, o_buf, in_sem.at[2 * count]))
    for copy in copies:
        copy.start()
    for copy in copies:
        copy.wait()
    core = meta[0]
    live = meta[1]

    def slot_of(place):
        part = place // half
        inner = lax.rem(place, half)
        owner = jnp.where(part == 0, 1 - core, core)
        return (inner // 4) * 8 + owner * 4 + lax.rem(inner, 4)

    def trip(step, carry):
        values = []
        for u in range(UNROLL):
            place = step * UNROLL + u
            slot = slot_of(place)
            row = pl.multiple_of(rows[slot] * 128, 128)
            col = pl.multiple_of(cols[slot] * 128, 128)
            value = lax.dot_general(
                x_buf[:, pl.ds(row, 128)],
                g_buf[:, pl.ds(col, 128)],
                (((0,), (0,)), ((), ())),
                preferred_element_type=jnp.float32,
            )
            if not first:
                value = jnp.where(slot < live, o_buf[place] + value, 0.0)
            values.append(value)
        for u in range(UNROLL):
            o_buf[step * UNROLL + u] = values[u]
        return carry

    lax.fori_loop(0, half // UNROLL, trip, 0)
    if first:
        outs = [
            pltpu.make_async_copy(o_buf.at[pl.ds(0, half)], out_hbm.at[pl.ds(0, half)], out_sem.at[0]),
            pltpu.make_async_copy(o_buf.at[pl.ds(half, half)], out_hbm.at[pl.ds(half, half)], out_sem.at[1]),
        ]
    else:
        outs = [
            pltpu.make_async_copy(o_buf.at[pl.ds(0, half)], send_hbm, out_sem.at[0]),
            pltpu.make_async_copy(o_buf.at[pl.ds(half, half)], keep_hbm, out_sem.at[1]),
        ]
    outs[0].start()
    lax.fori_loop(half // UNROLL, slots // UNROLL, trip, 0)
    outs[1].start()
    outs[0].wait()
    outs[1].wait()


def partial_grads(name, layout, meta, rows, cols, pieces, out_grad, acc=None):
    first = acc is None
    slots = rows.shape[0]
    depth = sum(size for _, _, size in layout)
    width = pieces[0].shape[1]
    any_spec = pl.BlockSpec(memory_space=pl.ANY)
    block = (slots, 128, 128)
    half = (slots // 2, 128, 128)
    if first:
        out_shape = jax.ShapeDtypeStruct(block, jnp.float32)
        out_specs = any_spec
        extra = ()
    else:
        out_shape = (jax.ShapeDtypeStruct(half, jnp.float32), jax.ShapeDtypeStruct(half, jnp.float32))
        out_specs = (any_spec, any_spec)
        extra = (acc,)
    return pl.pallas_call(
        functools.partial(grads_kernel, layout, first),
        name=name,
        out_shape=out_shape,
        in_specs=[pl.BlockSpec(memory_space=pltpu.SMEM)] * 3 + [any_spec] * (len(pieces) + 1 + len(extra)),
        out_specs=out_specs,
        scratch_shapes=[
            pltpu.VMEM((depth, width), jnp.bfloat16),
            pltpu.VMEM((depth, out_grad.shape[1]), jnp.bfloat16),
            pltpu.VMEM(block, jnp.float32),
            pltpu.SemaphoreType.DMA((2 * len(pieces) + 1,)),
            pltpu.SemaphoreType.DMA((2,)),
        ],
        compiler_params=pltpu.CompilerParams(vmem_limit_bytes=40 * 1024 * 1024),
        cost_estimate=pl.CostEstimate(
            flops=2 * slots * 128 * 128 * depth, bytes_accessed=30_000_000, transcendentals=0
        ),
    )(meta, rows, cols, *pieces, out_grad, *extra)


def on_device(tokens, out_grad, delta, block_rows, block_cols, block_count):
    slots = block_rows.shape[0]
    dp = lax.axis_index("dp")
    tp = lax.axis_index("tensor")
    across = lax.bitwise_xor(tp, 1)
    meta = jnp.stack(
        [
            lax.rem(dp, 2),
            block_count[0],
            tp,
            lax.rem(tp + 6, 8),
            lax.rem(tp + 2, 8),
            lax.rem(tp + 4, 8),
            across,
            lax.rem(across + 6, 8),
            lax.rem(across + 2, 8),
            lax.rem(across + 4, 8),
        ]
    ).astype(jnp.int32)
    OWN, BELOW, ABOVE, FAR, X_OWN, X_BELOW, X_ABOVE, X_FAR = range(2, 10)

    def move(value, pairs, axis="tensor"):
        return lax.ppermute(value, axis, pairs)

    part_a, part_b = tokens[:64], tokens[64:]
    with jax.named_scope("gather"):
        b_below, b_above = move(part_b, Y_UP), move(part_b, Y_DOWN)
        x_a = move(part_a, X_SWAP)
        a_below, a_above = move(part_a, Y_UP), move(part_a, Y_DOWN)
        x_b = move(part_b, X_SWAP)
        b_far = move(b_below[:32], Y_UP), move(b_above[32:], Y_DOWN)
        a_far = move(a_below[:32], Y_UP), move(a_above[32:], Y_DOWN)
        x_b_below, x_b_above = move(b_below, X_SWAP), move(b_above, X_SWAP)
        x_a_below, x_a_above = move(x_a, Y_UP), move(x_a, Y_DOWN)
        x_b_far = move(b_far[0], X_SWAP), move(b_far[1], X_SWAP)
        x_a_far = move(x_a_below[:32], Y_UP), move(x_a_above[32:], Y_DOWN)

    with jax.named_scope("bound"):
        top = jnp.broadcast_to(jnp.max(jnp.abs(out_grad)).astype(jnp.float32), (8, 128))
        for pairs in (CORE_SWAP, z_swap(1), z_swap(2), z_swap(4), X_HI_SWAP):
            top = jnp.maximum(top, move(top, pairs, "dp"))
        top = jnp.clip(top[0, 0], 1e-30, 1e37)
        shrink = 2.0 / top
        grow = 0.5 * top
        meta, shrink, grow = lax.optimization_barrier((meta, shrink, grow))

    own_layout = (
        (OWN, 0, 128),
        (BELOW, 0, 64), (ABOVE, 0, 64), (BELOW, 64, 64), (ABOVE, 64, 64),
        (FAR, 0, 32), (FAR, 32, 32), (FAR, 64, 32), (FAR, 96, 32),
    )
    acc = partial_grads(
        "own_column", own_layout, meta, block_rows, block_cols,
        (tokens, a_below, a_above, b_below, b_above, *a_far, *b_far), out_grad,
    )
    across_layout = (
        (X_OWN, 0, 64), (X_OWN, 64, 64),
        (X_BELOW, 0, 64), (X_ABOVE, 0, 64), (X_BELOW, 64, 64), (X_ABOVE, 64, 64),
        (X_FAR, 0, 32), (X_FAR, 32, 32), (X_FAR, 64, 32), (X_FAR, 96, 32),
    )
    send, keep = partial_grads(
        "across_column", across_layout, meta, block_rows, block_cols,
        (x_a, x_b, x_a_below, x_a_above, x_b_below, x_b_above, *x_a_far, *x_b_far), out_grad, acc,
    )
    with jax.named_scope("reduce"):
        summed = keep + move(send, CORE_SWAP, "dp")
        packed = (summed * shrink).astype(jnp.float16)
        swapped = lax.all_to_all(packed, "dp", 0, 0, axis_index_groups=SAME_CORE, tiled=True)
        share = delta.shape[1]
        grads = jnp.sum(swapped.reshape(-1, share, 128, 128).astype(jnp.float32), axis=0) * grow
    with jax.named_scope("norm"):
        square_sum = jnp.broadcast_to(jnp.sum(grads * grads), (8, 128))
        for pairs in (CORE_SWAP, z_swap(1), z_swap(2), z_swap(4), X_HI_SWAP):
            square_sum = square_sum + move(square_sum, pairs, "dp")
        for pairs in (X_SWAP, Y_UP):
            if pairs is Y_UP:
                one = square_sum + move(square_sum, [(t, t ^ 2) for t in range(8)])
                square_sum = one + move(one, [(t, t ^ 4) for t in range(8)])
            else:
                square_sum = square_sum + move(square_sum, pairs)
        square_sum = square_sum[0, 0]
    norm_limit = 128 * math.sqrt(8 * slots)
    factor = jnp.minimum(jnp.float32(1.0), norm_limit / jnp.sqrt(square_sum + 1e-06))
    return delta - 0.5 * factor * grads[None]


def solution(mesh):
    return jax.shard_map(
        on_device,
        mesh=mesh,
        in_specs=(
            P(("dp", "tensor"), None),
            P("dp", "tensor"),
            P("tensor", "dp", None, None),
            P("tensor"),
            P("tensor"),
            P("tensor"),
        ),
        out_specs=P("tensor", "dp", None, None),
        check_vma=False,
    )
```

```python
import functools
import math

import jax
import jax.numpy as jnp
from jax import lax
from jax.experimental import pallas as pl
from jax.experimental.pallas import tpu as pltpu
from jax.sharding import PartitionSpec as P


UNROLL = 8
X_SWAP = [(t, t ^ 1) for t in range(8)]
Y_UP = [(t, (t + 2) % 8) for t in range(8)]
Y_DOWN = [(t, (t + 6) % 8) for t in range(8)]
CORE_SWAP = [(d, d ^ 1) for d in range(32)]
X_HI_SWAP = [(d, d ^ 16) for d in range(32)]
DIAGONAL = [(d * 8 + t, (d ^ 16) * 8 + (t ^ 1)) for d in range(32) for t in range(8)]


def z_swap(bit):
    return [(d, d ^ (bit * 2)) for d in range(32)]


def z_shift(k):
    return [(d, (d // 16) * 16 + (d + 2 * k) % 16) for d in range(32)]


CORE, Z, X_HI, OWN, BELOW, ABOVE, FAR = range(7)


def grads_kernel(plan, depths, split, with_acc, meta, slots_ref, *refs):
    count = len(plan)
    pieces = refs[:count]
    at = count
    grads = refs[at : at + len(depths)]
    at += len(depths)
    if with_acc:
        acc_hbm = refs[at]
        at += 1
    outs_hbm = refs[at : at + (2 if split else 1)]
    at += len(outs_hbm)
    x_buf, g_buf, o_buf, in_sem, out_sem = refs[at:]
    places = o_buf.shape[0]
    half = places // 2
    copies = []
    row = 0
    for index, size in enumerate(plan):
        copies.append(
            pltpu.make_async_copy(pieces[index], x_buf.at[pl.ds(row, size), :], in_sem.at[len(copies)])
        )
        row += size
    row = 0
    for index, (size, source) in enumerate(depths):
        block = grads[index]
        if source is not None:
            block = block.at[pl.ds(pl.multiple_of(meta[source] * 128, 128), size), :]
        copies.append(
            pltpu.make_async_copy(block, g_buf.at[pl.ds(row, size), :], in_sem.at[len(copies)])
        )
        row += size
    if with_acc:
        copies.append(pltpu.make_async_copy(acc_hbm, o_buf, in_sem.at[len(copies)]))
    for copy in copies:
        copy.start()
    for copy in copies:
        copy.wait()
    core, z, x_hi = meta[CORE], meta[Z], meta[X_HI]
    live = slots_ref[2, 0]

    def slot_of(place):
        part = lax.shift_right_logical(place, 6)
        far_half = lax.bitwise_and(lax.shift_right_logical(place, 5), 1)
        ahead = lax.bitwise_and(lax.shift_right_logical(place, 2), 7)
        owner_core = lax.bitwise_xor(core, 1 - part)
        owner_x = lax.bitwise_xor(x_hi, far_half)
        owner_z = lax.bitwise_and(z + ahead, 7)
        return owner_x * 64 + owner_z * 8 + owner_core * 4 + lax.bitwise_and(place, 3)

    def trip(step, carry):
        values = []
        for u in range(UNROLL):
            place = step * UNROLL + u
            slot = slot_of(place)
            row = pl.multiple_of(slots_ref[0, slot] * 128, 128)
            col = pl.multiple_of(slots_ref[1, slot] * 128, 128)
            value = lax.dot_general(
                x_buf[:, pl.ds(row, 128)],
                g_buf[:, pl.ds(col, 128)],
                (((0,), (0,)), ((), ())),
                preferred_element_type=jnp.float32,
            )
            if with_acc:
                value = o_buf[place] + value
            if split:
                value = jnp.where(slot < live, value, 0.0)
            values.append(value)
        for u in range(UNROLL):
            o_buf[step * UNROLL + u] = values[u]
        return carry

    if split:
        targets = outs_hbm
    else:
        targets = [outs_hbm[0].at[pl.ds(0, half)], outs_hbm[0].at[pl.ds(half, half)]]
    outs = [
        pltpu.make_async_copy(o_buf.at[pl.ds(i * half, half)], targets[i], out_sem.at[i]) for i in range(2)
    ]
    lax.fori_loop(0, half // UNROLL, trip, 0)
    outs[0].start()
    lax.fori_loop(half // UNROLL, places // UNROLL, trip, 0)
    outs[1].start()
    outs[0].wait()
    outs[1].wait()


def partial_grads(meta, slot_table, pieces, grads, sources, split, acc=None):
    plan = tuple(piece.shape[0] for piece in pieces)
    depth = sum(plan)
    depths = tuple((128, source) for source in sources)
    assert depth == 128 * len(depths)
    places = slot_table.shape[1]
    any_spec = pl.BlockSpec(memory_space=pl.ANY)
    block = (places, 128, 128)
    half = jax.ShapeDtypeStruct((places // 2, 128, 128), jnp.float32)
    out_shape = (half, half) if split else (jax.ShapeDtypeStruct(block, jnp.float32),)
    extra = () if acc is None else (acc,)
    operands = (*pieces, *grads, *extra)
    return pl.pallas_call(
        functools.partial(grads_kernel, plan, depths, split, acc is not None),
        out_shape=out_shape,
        in_specs=[pl.BlockSpec(memory_space=pltpu.SMEM)] * 2 + [any_spec] * len(operands),
        out_specs=tuple(any_spec for _ in out_shape),
        scratch_shapes=[
            pltpu.VMEM((depth, pieces[0].shape[1]), jnp.bfloat16),
            pltpu.VMEM((depth, grads[0].shape[1]), jnp.bfloat16),
            pltpu.VMEM(block, jnp.float32),
            pltpu.SemaphoreType.DMA((len(operands),)),
            pltpu.SemaphoreType.DMA((2,)),
        ],
        compiler_params=pltpu.CompilerParams(vmem_limit_bytes=56 * 1024 * 1024),
        cost_estimate=pl.CostEstimate(
            flops=2 * places * 128 * 128 * depth, bytes_accessed=30_000_000, transcendentals=0
        ),
    )(meta, slot_table, *operands)


def on_device(tokens, out_grad, delta, block_rows, block_cols, block_count):
    places = block_rows.shape[0]
    dp = lax.axis_index("dp")
    tp = lax.axis_index("tensor")
    across = lax.bitwise_xor(tp, 1)

    def around(base):
        return [base, lax.bitwise_and(base + 6, 7), lax.bitwise_and(base + 2, 7), lax.bitwise_and(base + 4, 7)]

    def move(value, pairs, axis="tensor"):
        return lax.ppermute(value, axis, pairs)

    meta = jnp.stack(
        [lax.bitwise_and(dp, 1), lax.bitwise_and(dp >> 1, 7), dp >> 4, *around(tp)]
    ).astype(jnp.int32)
    table = jnp.stack([block_rows, block_cols, jnp.broadcast_to(block_count, (places,))])
    part_a, part_b = tokens[:64], tokens[64:]
    theirs = [lax.dynamic_slice_in_dim(out_grad, chunk * 128, 128, 0) for chunk in around(across)]
    below_a, above_b = move(part_a, Y_UP), move(part_b, Y_DOWN)
    table_x = move(table, X_SWAP)
    top = jnp.broadcast_to(jnp.max(jnp.abs(out_grad)).astype(jnp.float32), (8, 128))
    for pairs, axis in (
        (X_SWAP, "tensor"),
        (X_HI_SWAP, "dp"),
        (CORE_SWAP, "dp"),
        (z_swap(1), "dp"),
        (z_swap(2), "dp"),
        (z_swap(4), "dp"),
    ):
        top = jnp.maximum(top, move(top, pairs, axis))
    top = jnp.clip(top[0, 0], 1e-30, 1e37)
    g_own = move(theirs[0], X_SWAP)
    below_b, above_a = move(part_b, Y_UP), move(part_a, Y_DOWN)
    g_below = move(theirs[1], X_SWAP)
    g_above = move(theirs[2], X_SWAP)
    g_far = move(theirs[3], X_SWAP)
    far_a, far_b = move(below_a, Y_UP), move(above_b, Y_DOWN)
    meta_late, shrink, grow = lax.optimization_barrier((meta, 0.25 / top, 4.0 * top))

    (acc,) = partial_grads(
        meta, table_x, (tokens, below_a, below_b, above_a, above_b),
        (g_own, g_below, g_above), (None, None, None), False,
    )
    send, keep = partial_grads(
        meta_late, table, (tokens, below_a, below_b, above_a, above_b, far_a, far_b),
        (out_grad, out_grad, out_grad, out_grad), (OWN, BELOW, ABOVE, FAR), True,
    )
    send_x, keep_x = partial_grads(meta, table_x, (far_a, far_b), (g_far,), (None,), True, acc)
    share = delta.shape[1]
    quarter = places // 4
    ours = (keep + move(send, CORE_SWAP, "dp")) * shrink
    far_half = move(ours[quarter:].astype(jnp.float16), X_HI_SWAP, "dp")
    other = ((keep_x + move(send_x, CORE_SWAP, "dp")) * shrink).astype(jnp.float16)
    near_x = move(other[:quarter], X_SWAP)
    far_x = move(other[quarter:], DIAGONAL, ("dp", "tensor"))
    ours = (
        ours[:quarter]
        + far_half.astype(jnp.float32)
        + near_x.astype(jnp.float32)
        + far_x.astype(jnp.float32)
    )
    packed = ours.astype(jnp.float16)
    grads = ours[:share]
    for k in (4, 3, 5, 2, 6, 1, 7):
        got = move(packed[share * k : share * (k + 1)], z_shift(k), "dp")
        grads = grads + got.astype(jnp.float32)
    grads = grads * grow
    square_sum = jnp.broadcast_to(jnp.sum(grads * grads), (8, 128))
    for axis, size in (("dp", 32), ("tensor", 8)):
        spread = jnp.broadcast_to(square_sum[None], (size, 8, 128))
        square_sum = jnp.sum(lax.all_to_all(spread, axis, 0, 0, tiled=True), axis=0)
    square_sum = square_sum[0, 0]
    norm_limit = 128 * math.sqrt(8 * places)
    factor = jnp.minimum(jnp.float32(1.0), norm_limit / jnp.sqrt(square_sum + 1e-06))
    return delta - 0.5 * factor * grads[None]


def solution(mesh):
    return jax.shard_map(
        on_device,
        mesh=mesh,
        in_specs=(
            P(("dp", "tensor"), None),
            P("dp", "tensor"),
            P("tensor", "dp", None, None),
            P("tensor"),
            P("tensor"),
            P("tensor"),
        ),
        out_specs=P("tensor", "dp", None, None),
        check_vma=False,
    )
```

```python
import functools
import math

import jax
import jax.numpy as jnp
from jax import lax
from jax.experimental import pallas as pl
from jax.experimental.pallas import tpu as pltpu
from jax.sharding import PartitionSpec as P


UNROLL = 8
CHUNKS = 4
X_SWAP = [(t, t ^ 1) for t in range(8)]
Y_UP = [(t, (t + 2) % 8) for t in range(8)]
Y_DOWN = [(t, (t + 6) % 8) for t in range(8)]
CORE_SWAP = [(d, d ^ 1) for d in range(32)]
X_HI_SWAP = [(d, d ^ 16) for d in range(32)]
DIAGONAL = [(d * 8 + t, (d ^ 16) * 8 + (t ^ 1)) for d in range(32) for t in range(8)]


def z_swap(bit):
    return [(d, d ^ (bit * 2)) for d in range(32)]


def z_shift(k):
    return [(d, (d // 16) * 16 + (d + 2 * k) % 16) for d in range(32)]


CORE, Z, X_HI, OWN, BELOW, ABOVE, FAR = range(7)


def grads_kernel(plan, depths, split, with_acc, meta, slots_ref, *refs):
    count = len(plan)
    pieces = refs[:count]
    at = count
    grads = refs[at : at + len(depths)]
    at += len(depths)
    if with_acc:
        acc_hbm = refs[at]
        at += 1
    outs_hbm = refs[at : at + (2 if split else 1)]
    at += len(outs_hbm)
    x_buf, g_buf, o_buf, in_sem, out_sem = refs[at:]
    places = o_buf.shape[0]
    copies = []
    row = 0
    for index, size in enumerate(plan):
        copies.append(
            pltpu.make_async_copy(pieces[index], x_buf.at[pl.ds(row, size), :], in_sem.at[len(copies)])
        )
        row += size
    row = 0
    for index, (size, source) in enumerate(depths):
        block = grads[index]
        if source is not None:
            block = block.at[pl.ds(pl.multiple_of(meta[source] * 128, 128), size), :]
        copies.append(
            pltpu.make_async_copy(block, g_buf.at[pl.ds(row, size), :], in_sem.at[len(copies)])
        )
        row += size
    piece = places // CHUNKS
    loads = []
    if with_acc:
        loads = [
            pltpu.make_async_copy(
                acc_hbm.at[pl.ds(i * piece, piece)],
                o_buf.at[pl.ds(i * piece, piece)],
                in_sem.at[len(copies) + i],
            )
            for i in range(CHUNKS)
        ]
    for copy in copies + loads:
        copy.start()
    for copy in copies:
        copy.wait()
    core, z, x_hi = meta[CORE], meta[Z], meta[X_HI]
    live = slots_ref[2, 0]

    def slot_of(place):
        part = lax.shift_right_logical(place, 6)
        far_half = lax.bitwise_and(lax.shift_right_logical(place, 5), 1)
        ahead = lax.bitwise_and(lax.shift_right_logical(place, 2), 7)
        owner_core = lax.bitwise_xor(core, 1 - part)
        owner_x = lax.bitwise_xor(x_hi, far_half)
        owner_z = lax.bitwise_and(z + ahead, 7)
        return owner_x * 64 + owner_z * 8 + owner_core * 4 + lax.bitwise_and(place, 3)

    def trip(step, carry):
        values = []
        for u in range(UNROLL):
            place = step * UNROLL + u
            slot = slot_of(place)
            row = pl.multiple_of(slots_ref[0, slot] * 128, 128)
            col = pl.multiple_of(slots_ref[1, slot] * 128, 128)
            value = lax.dot_general(
                x_buf[:, pl.ds(row, 128)],
                g_buf[:, pl.ds(col, 128)],
                (((0,), (0,)), ((), ())),
                preferred_element_type=jnp.float32,
            )
            if with_acc:
                value = o_buf[place] + value
            if split:
                value = jnp.where(slot < live, value, 0.0)
            values.append(value)
        for u in range(UNROLL):
            o_buf[step * UNROLL + u] = values[u]
        return carry

    stores = []
    for i in range(CHUNKS):
        target = outs_hbm[i * len(outs_hbm) // CHUNKS]
        start = i % (CHUNKS // len(outs_hbm)) * piece
        stores.append(
            pltpu.make_async_copy(
                o_buf.at[pl.ds(i * piece, piece)], target.at[pl.ds(start, piece)], out_sem.at[i]
            )
        )
    for i in range(CHUNKS):
        if loads:
            loads[i].wait()
        lax.fori_loop(i * piece // UNROLL, (i + 1) * piece // UNROLL, trip, 0)
        stores[i].start()
    for store in stores:
        store.wait()


def partial_grads(meta, slot_table, pieces, grads, sources, split, acc=None):
    plan = tuple(piece.shape[0] for piece in pieces)
    depth = sum(plan)
    depths = tuple((128, source) for source in sources)
    assert depth == 128 * len(depths)
    places = slot_table.shape[1]
    any_spec = pl.BlockSpec(memory_space=pl.ANY)
    block = (places, 128, 128)
    half = jax.ShapeDtypeStruct((places // 2, 128, 128), jnp.float32)
    out_shape = (half, half) if split else (jax.ShapeDtypeStruct(block, jnp.float32),)
    extra = () if acc is None else (acc,)
    operands = (*pieces, *grads, *extra)
    return pl.pallas_call(
        functools.partial(grads_kernel, plan, depths, split, acc is not None),
        out_shape=out_shape,
        in_specs=[pl.BlockSpec(memory_space=pltpu.SMEM)] * 2 + [any_spec] * len(operands),
        out_specs=tuple(any_spec for _ in out_shape),
        scratch_shapes=[
            pltpu.VMEM((depth, pieces[0].shape[1]), jnp.bfloat16),
            pltpu.VMEM((depth, grads[0].shape[1]), jnp.bfloat16),
            pltpu.VMEM(block, jnp.float32),
            pltpu.SemaphoreType.DMA((len(operands) + CHUNKS,)),
            pltpu.SemaphoreType.DMA((CHUNKS,)),
        ],
        compiler_params=pltpu.CompilerParams(vmem_limit_bytes=56 * 1024 * 1024),
        cost_estimate=pl.CostEstimate(
            flops=2 * places * 128 * 128 * depth, bytes_accessed=30_000_000, transcendentals=0
        ),
    )(meta, slot_table, *operands)


def on_device(tokens, out_grad, delta, block_rows, block_cols, block_count):
    places = block_rows.shape[0]
    dp = lax.axis_index("dp")
    tp = lax.axis_index("tensor")
    across = lax.bitwise_xor(tp, 1)

    def around(base):
        return [base, lax.bitwise_and(base + 6, 7), lax.bitwise_and(base + 2, 7), lax.bitwise_and(base + 4, 7)]

    def move(value, pairs, axis="tensor"):
        return lax.ppermute(value, axis, pairs)

    meta = jnp.stack(
        [lax.bitwise_and(dp, 1), lax.bitwise_and(dp >> 1, 7), dp >> 4, *around(tp)]
    ).astype(jnp.int32)
    table = jnp.stack([block_rows, block_cols, jnp.broadcast_to(block_count, (places,))])
    chunks = around(across)

    def theirs(source, index):
        return lax.dynamic_slice_in_dim(source, chunks[index] * 128, 128, 0)

    below, above = move(tokens, Y_UP), move(tokens, Y_DOWN)
    first_rows, later = lax.optimization_barrier((theirs(out_grad, 0), out_grad))
    g_own = move(first_rows, X_SWAP)
    table_x = move(table, X_SWAP)
    g_below, g_above, g_far = (
        move(theirs(later, i), X_SWAP) for i in (1, 2, 3)
    )
    far_a, far_b = move(below[:64], Y_UP), move(above[64:], Y_DOWN)
    top = jnp.broadcast_to(jnp.max(jnp.abs(later)).astype(jnp.float32), (8, 128))
    for pairs, axis in (
        (CORE_SWAP, "dp"),
        (z_swap(1), "dp"),
        (z_swap(2), "dp"),
        (z_swap(4), "dp"),
        (X_SWAP, "tensor"),
        (X_HI_SWAP, "dp"),
    ):
        top = jnp.maximum(top, move(top, pairs, axis))
    top = jnp.clip(top[0, 0], 1e-30, 1e37)
    meta_late, shrink, grow = lax.optimization_barrier((meta, 0.25 / top, 4.0 * top))

    near = (tokens, below, above)
    far = (far_a, far_b)
    (acc,) = partial_grads(meta, table, near, (out_grad,) * 3, (OWN, BELOW, ABOVE), False)
    (acc_x,) = partial_grads(meta, table_x, near, (g_own, g_below, g_above), (None,) * 3, False)
    send, keep = partial_grads(meta_late, table, far, (out_grad,), (FAR,), True, acc)
    send_x, keep_x = partial_grads(meta_late, table_x, far, (g_far,), (None,), True, acc_x)

    share = delta.shape[1]
    quarter = places // 4

    def z_sum(value):
        packed = value.astype(jnp.float16)
        total = value[:share]
        for k in (4, 3, 5, 2, 6, 1, 7):
            got = move(packed[share * k : share * (k + 1)], z_shift(k), "dp")
            total = total + got.astype(jnp.float32)
        return total

    own_back = move(send, CORE_SWAP, "dp")
    own_sum = (keep + own_back) * shrink
    other = ((keep_x + move(send_x, CORE_SWAP, "dp")) * shrink).astype(jnp.float16)
    near_x = move(other[:quarter], X_SWAP)
    far_x = move(other[quarter:], DIAGONAL, ("dp", "tensor"))
    from_far = move(z_sum(own_sum[quarter:]), X_HI_SWAP, "dp")
    ours = own_sum[:quarter] + near_x.astype(jnp.float32) + far_x.astype(jnp.float32)
    grads = (z_sum(ours) + from_far) * grow
    square_sum = jnp.broadcast_to(jnp.sum(grads * grads), (8, 128))
    for axis, size in (("dp", 32), ("tensor", 8)):
        spread = jnp.broadcast_to(square_sum[None], (size, 8, 128))
        square_sum = jnp.sum(lax.all_to_all(spread, axis, 0, 0, tiled=True), axis=0)
    square_sum = square_sum[0, 0]
    norm_limit = 128 * math.sqrt(8 * places)
    factor = jnp.minimum(jnp.float32(1.0), norm_limit / jnp.sqrt(square_sum + 1e-06))
    return delta - 0.5 * factor * grads[None]


def solution(mesh):
    return jax.shard_map(
        on_device,
        mesh=mesh,
        in_specs=(
            P(("dp", "tensor"), None),
            P("dp", "tensor"),
            P("tensor", "dp", None, None),
            P("tensor"),
            P("tensor"),
            P("tensor"),
        ),
        out_specs=P("tensor", "dp", None, None),
        check_vma=False,
    )
```

```python
import functools
import math

import jax
import jax.numpy as jnp
from jax import lax
from jax.experimental import pallas as pl
from jax.experimental.pallas import tpu as pltpu
from jax.sharding import PartitionSpec as P


CHUNK = 32
X_SWAP = [(t, t ^ 1) for t in range(8)]
Y_UP = [(t, (t + 2) % 8) for t in range(8)]
Y_DOWN = [(t, (t + 6) % 8) for t in range(8)]
CORE_SWAP = [(d, d ^ 1) for d in range(32)]
X_HI_SWAP = [(d, d ^ 16) for d in range(32)]
DIAGONAL = [(d * 8 + t, (d ^ 16) * 8 + (t ^ 1)) for d in range(32) for t in range(8)]


Z_GROUPS = [[xh * 16 + z * 2 + c for z in range(8)] for xh in range(2) for c in range(2)]


def z_swap(bit):
    return [(d, d ^ (bit * 2)) for d in range(32)]


def z_shift(k):
    return [(d, (d // 16) * 16 + (d + 2 * k) % 16) for d in range(32)]


Z_STEPS = (4, 3, 5, 2, 6, 1, 7)
CORE, Z, X_HI, OWN, BELOW, ABOVE, FAR = range(7)


def grads_kernel(plan, depths, split, with_acc, own, meta, slots_ref, *refs):
    count = len(plan)
    pieces = refs[:count]
    at = count
    grads = refs[at : at + len(depths)]
    at += len(depths)
    if with_acc:
        acc_hbm = refs[at]
        at += 1
    outs_hbm = refs[at : at + (2 if split else 1)]
    at += len(outs_hbm)
    x_buf, g_buf, o_buf, in_sem, acc_sem, out_sem = refs[at:]
    places = o_buf.shape[0]
    copies = []
    row = 0
    for index, size in enumerate(plan):
        copies.append(
            pltpu.make_async_copy(pieces[index], x_buf.at[pl.ds(row, size), :], in_sem.at[len(copies)])
        )
        row += size
    row = 0
    for index, (size, source) in enumerate(depths):
        block = grads[index]
        if source is not None:
            block = block.at[pl.ds(pl.multiple_of(meta[source] * 128, 128), size), :]
        copies.append(
            pltpu.make_async_copy(block, g_buf.at[pl.ds(row, size), :], in_sem.at[len(copies)])
        )
        row += size
    chunks = places // CHUNK
    unroll = CHUNK // 2 if with_acc else CHUNK

    def acc_load(i):
        span = pl.ds(i * CHUNK, CHUNK)
        return pltpu.make_async_copy(acc_hbm.at[span], o_buf.at[span], acc_sem.at[i])

    def store(target, start, i):
        return pltpu.make_async_copy(
            o_buf.at[pl.ds(i * CHUNK, CHUNK)], target.at[pl.ds(start * CHUNK, CHUNK)], out_sem.at[i]
        )

    for copy in copies:
        copy.start()
    if with_acc:
        for i in range(chunks):
            acc_load(i).start()
    for copy in copies:
        copy.wait()
    core, z, x_hi = meta[CORE], meta[Z], meta[X_HI]
    live = slots_ref[2, 0]

    def slot_of(place):
        part = lax.shift_right_logical(place, 6)
        far_half = lax.bitwise_and(lax.shift_right_logical(place, 5), 1)
        ahead = lax.bitwise_and(lax.shift_right_logical(place, 2), 7)
        owner_core = lax.bitwise_xor(core, 1 - part)
        owner_x = lax.bitwise_xor(x_hi, far_half)
        owner_z = lax.bitwise_and((z * (1 - far_half) if own else z) + ahead, 7)
        return owner_x * 64 + owner_z * 8 + owner_core * 4 + lax.bitwise_and(place, 3)

    def trip(step, carry):
        values = []
        for u in range(unroll):
            place = step * unroll + u
            slot = slot_of(place)
            row = pl.multiple_of(slots_ref[0, slot] * 128, 128)
            col = pl.multiple_of(slots_ref[1, slot] * 128, 128)
            value = lax.dot_general(
                x_buf[:, pl.ds(row, 128)],
                g_buf[:, pl.ds(col, 128)],
                (((0,), (0,)), ((), ())),
                preferred_element_type=jnp.float32,
            )
            if with_acc:
                value = o_buf[place] + value
            if split:
                value = jnp.where(slot < live, value, 0.0)
            values.append(value)
        for u in range(unroll):
            o_buf[step * unroll + u] = values[u]
        return carry

    each = CHUNK // unroll

    def chunk(i, carry):
        lax.fori_loop(i * each, (i + 1) * each, trip, 0)
        store(outs_hbm[0], i, i).start()
        return carry

    if split:
        stores = [store(outs_hbm[i * 2 // chunks], i % (chunks // 2), i) for i in range(chunks)]
        for i in range(chunks):
            if with_acc:
                acc_load(i).wait()
            lax.fori_loop(i * each, (i + 1) * each, trip, 0)
            stores[i].start()
    else:
        stores = [store(outs_hbm[0], i, i) for i in range(chunks)]
        lax.fori_loop(0, chunks, chunk, 0)
    for copy in stores:
        copy.wait()


def partial_grads(name, meta, slot_table, pieces, grads, sources, split, acc=None):
    plan = tuple(piece.shape[0] for piece in pieces)
    depth = sum(plan)
    depths = tuple((128, source) for source in sources)
    assert depth == 128 * len(depths)
    places = slot_table.shape[1]
    any_spec = pl.BlockSpec(memory_space=pl.ANY)
    block = (places, 128, 128)
    half = jax.ShapeDtypeStruct((places // 2, 128, 128), jnp.float32)
    out_shape = (half, half) if split else (jax.ShapeDtypeStruct(block, jnp.float32),)
    extra = () if acc is None else (acc,)
    operands = (*pieces, *grads, *extra)
    return pl.pallas_call(
        functools.partial(grads_kernel, plan, depths, split, acc is not None, name.startswith("own")),
        out_shape=out_shape,
        in_specs=[pl.BlockSpec(memory_space=pltpu.SMEM)] * 2 + [any_spec] * len(operands),
        out_specs=tuple(any_spec for _ in out_shape),
        scratch_shapes=[
            pltpu.VMEM((depth, pieces[0].shape[1]), jnp.bfloat16),
            pltpu.VMEM((depth, grads[0].shape[1]), jnp.bfloat16),
            pltpu.VMEM(block, jnp.float32),
            pltpu.SemaphoreType.DMA((len(operands),)),
            pltpu.SemaphoreType.DMA((places // CHUNK,)),
            pltpu.SemaphoreType.DMA((places // CHUNK,)),
        ],
        compiler_params=pltpu.CompilerParams(vmem_limit_bytes=56 * 1024 * 1024),
        cost_estimate=pl.CostEstimate(
            flops=2 * places * 128 * 128 * depth, bytes_accessed=30_000_000, transcendentals=0
        ),
    )(meta, slot_table, *operands)


def on_device(tokens, out_grad, delta, block_rows, block_cols, block_count):
    places = block_rows.shape[0]
    dp = lax.axis_index("dp")
    tp = lax.axis_index("tensor")
    across = lax.bitwise_xor(tp, 1)

    def around(base):
        return [base, lax.bitwise_and(base + 6, 7), lax.bitwise_and(base + 2, 7), lax.bitwise_and(base + 4, 7)]

    def move(value, pairs, axis="tensor"):
        return lax.ppermute(value, axis, pairs)

    meta = jnp.stack(
        [lax.bitwise_and(dp, 1), lax.bitwise_and(dp >> 1, 7), dp >> 4, *around(tp)]
    ).astype(jnp.int32)
    table = jnp.stack([block_rows, block_cols, jnp.broadcast_to(block_count, (places,))])
    chunks = around(across)

    def theirs(source, index):
        return lax.dynamic_slice_in_dim(source, chunks[index] * 128, 128, 0)

    part_a, part_b = tokens[:64], tokens[64:]
    below_a, above_b = move(part_a, Y_UP), move(part_b, Y_DOWN)
    below_b, above_a = move(part_b, Y_UP), move(part_a, Y_DOWN)
    first_rows, later = lax.optimization_barrier((theirs(out_grad, 0), out_grad))
    g_own = move(first_rows, X_SWAP)
    table_x = move(table, X_SWAP)
    g_below, g_above, g_far = (
        move(theirs(later, i), X_SWAP) for i in (1, 2, 3)
    )
    far_a, far_b = move(below_a, Y_UP), move(above_b, Y_DOWN)
    top = jnp.broadcast_to(jnp.max(jnp.abs(later)).astype(jnp.float32), (8, 128))
    for pairs, axis in (
        (CORE_SWAP, "dp"),
        (z_swap(1), "dp"),
        (z_swap(2), "dp"),
        (z_swap(4), "dp"),
        (X_SWAP, "tensor"),
        (X_HI_SWAP, "dp"),
    ):
        top = jnp.maximum(top, move(top, pairs, axis))
    top = jnp.clip(top[0, 0], 1e-30, 1e37)
    meta_late, shrink, grow = lax.optimization_barrier((meta, 0.25 / top, 4.0 * top))

    near = (tokens, below_a, below_b, above_a, above_b)
    far = (far_a, far_b)
    (acc,) = partial_grads(
        "own_near", meta, table, near, (out_grad,) * 3, (OWN, BELOW, ABOVE), False
    )
    (acc_x,) = partial_grads(
        "across_near", meta, table_x, near, (g_own, g_below, g_above), (None,) * 3, False
    )
    send, keep = partial_grads("own_far", meta_late, table, far, (out_grad,), (FAR,), True, acc)
    send_x, keep_x = partial_grads("across_far", meta_late, table_x, far, (g_far,), (None,), True, acc_x)

    share = delta.shape[1]
    quarter = places // 4

    def z_sum(value):
        packed = value.astype(jnp.float16)
        total = value[:share]
        for k in Z_STEPS:
            got = move(packed[share * k : share * (k + 1)], z_shift(k), "dp")
            total = total + got.astype(jnp.float32)
        return total

    own_back = move(send, CORE_SWAP, "dp")
    own_sum = lax.optimization_barrier((keep + own_back) * shrink)
    other = ((keep_x + move(send_x, CORE_SWAP, "dp")) * shrink).astype(jnp.float16)
    near_x = move(other[:quarter], X_SWAP)
    far_x = move(other[quarter:], DIAGONAL, ("dp", "tensor"))
    own_near, own_packed = lax.optimization_barrier(
        (own_sum[:quarter], own_sum[quarter:].astype(jnp.float16))
    )
    pieces = lax.all_to_all(own_packed, "dp", 0, 0, axis_index_groups=Z_GROUPS, tiled=True)
    pieces = jnp.sum(pieces.reshape(-1, share, 128, 128).astype(jnp.float32), axis=0)
    from_far = move(pieces, X_HI_SWAP, "dp")
    ours = own_near + near_x.astype(jnp.float32) + far_x.astype(jnp.float32)
    grads = (z_sum(ours) + from_far) * grow
    square_sum = jnp.broadcast_to(jnp.sum(grads * grads), (8, 128))
    for axis, size in (("dp", 32), ("tensor", 8)):
        spread = jnp.broadcast_to(square_sum[None], (size, 8, 128))
        square_sum = jnp.sum(lax.all_to_all(spread, axis, 0, 0, tiled=True), axis=0)
    square_sum = square_sum[0, 0]
    norm_limit = 128 * math.sqrt(8 * places)
    factor = jnp.minimum(jnp.float32(1.0), norm_limit / jnp.sqrt(square_sum + 1e-06))
    return delta - 0.5 * factor * grads[None]


def solution(mesh):
    return jax.shard_map(
        on_device,
        mesh=mesh,
        in_specs=(
            P(("dp", "tensor"), None),
            P("dp", "tensor"),
            P("tensor", "dp", None, None),
            P("tensor"),
            P("tensor"),
            P("tensor"),
        ),
        out_specs=P("tensor", "dp", None, None),
        check_vma=False,
    )
```

```python
import functools
import math

import jax
import jax.numpy as jnp
from jax import lax
from jax.experimental import pallas as pl
from jax.experimental.pallas import tpu as pltpu
from jax.sharding import PartitionSpec as P


CHUNK = 32
X_SWAP = [(t, t ^ 1) for t in range(8)]
Y_UP = [(t, (t + 2) % 8) for t in range(8)]
Y_DOWN = [(t, (t + 6) % 8) for t in range(8)]
CORE_SWAP = [(d, d ^ 1) for d in range(32)]
X_HI_SWAP = [(d, d ^ 16) for d in range(32)]
DIAGONAL = [(d * 8 + t, (d ^ 16) * 8 + (t ^ 1)) for d in range(32) for t in range(8)]


Z_GROUPS = [[xh * 16 + z * 2 + c for z in range(8)] for xh in range(2) for c in range(2)]


def z_swap(bit):
    return [(d, d ^ (bit * 2)) for d in range(32)]


def z_shift(k):
    return [(d, (d // 16) * 16 + (d + 2 * k) % 16) for d in range(32)]


Z_STEPS = (4, 3, 5, 2, 6, 1, 7)
CORE, Z, X_HI, OWN, BELOW, ABOVE, FAR = range(7)


def grads_kernel(plan, depths, split, with_acc, own, meta, slots_ref, *refs):
    count = len(plan)
    pieces = refs[:count]
    at = count
    grads = refs[at : at + len(depths)]
    at += len(depths)
    if with_acc:
        acc_hbm = refs[at]
        at += 1
    outs_hbm = refs[at : at + (2 if split else 1)]
    at += len(outs_hbm)
    x_buf, g_buf, o_buf, in_sem, acc_sem, out_sem = refs[at:]
    places = o_buf.shape[0]
    copies = []
    row = 0
    for index, size in enumerate(plan):
        copies.append(
            pltpu.make_async_copy(pieces[index], x_buf.at[pl.ds(row, size), :], in_sem.at[len(copies)])
        )
        row += size
    row = 0
    for index, (size, source) in enumerate(depths):
        block = grads[index]
        if source is not None:
            block = block.at[pl.ds(pl.multiple_of(meta[source] * 128, 128), size), :]
        copies.append(
            pltpu.make_async_copy(block, g_buf.at[pl.ds(row, size), :], in_sem.at[len(copies)])
        )
        row += size
    chunks = places // CHUNK
    unroll = CHUNK // 4 if with_acc else CHUNK // 2

    def acc_load(i):
        span = pl.ds(i * CHUNK, CHUNK)
        return pltpu.make_async_copy(acc_hbm.at[span], o_buf.at[span], acc_sem.at[i])

    def store(target, start, i):
        return pltpu.make_async_copy(
            o_buf.at[pl.ds(i * CHUNK, CHUNK)], target.at[pl.ds(start * CHUNK, CHUNK)], out_sem.at[i]
        )

    for copy in copies:
        copy.start()
    if with_acc:
        for i in range(chunks):
            acc_load(i).start()
    for copy in copies:
        copy.wait()
    core, z, x_hi = meta[CORE], meta[Z], meta[X_HI]
    live = slots_ref[2, 0]

    def slot_of(place):
        part = lax.shift_right_logical(place, 6)
        far_half = lax.bitwise_and(lax.shift_right_logical(place, 5), 1)
        ahead = lax.bitwise_and(lax.shift_right_logical(place, 1), 7)
        item = lax.bitwise_and(lax.shift_right_logical(place, 4), 1) * 2 + lax.bitwise_and(place, 1)
        if own:
            ahead = jnp.where(
                far_half == 1, lax.bitwise_and(lax.shift_right_logical(place, 2), 7), ahead
            )
            item = jnp.where(far_half == 1, lax.bitwise_and(place, 3), item)
        owner_core = lax.bitwise_xor(core, 1 - part)
        owner_x = lax.bitwise_xor(x_hi, far_half)
        owner_z = lax.bitwise_and((z * (1 - far_half) if own else z) + ahead, 7)
        return owner_x * 64 + owner_z * 8 + owner_core * 4 + item

    def trip(step, carry):
        values = []
        for u in range(unroll):
            place = step * unroll + u
            slot = slot_of(place)
            row = pl.multiple_of(slots_ref[0, slot] * 128, 128)
            col = pl.multiple_of(slots_ref[1, slot] * 128, 128)
            value = lax.dot_general(
                x_buf[:, pl.ds(row, 128)],
                g_buf[:, pl.ds(col, 128)],
                (((0,), (0,)), ((), ())),
                preferred_element_type=jnp.float32,
            )
            if with_acc:
                value = o_buf[place] + value
            if split:
                value = jnp.where(slot < live, value, 0.0)
            values.append(value)
        for u in range(unroll):
            o_buf[step * unroll + u] = values[u]
        return carry

    each = CHUNK // unroll

    def chunk(i, carry):
        lax.fori_loop(i * each, (i + 1) * each, trip, 0)
        store(outs_hbm[0], i, i).start()
        return carry

    if split:
        stores = [store(outs_hbm[i * 2 // chunks], i % (chunks // 2), i) for i in range(chunks)]
        for i in range(chunks):
            if with_acc:
                acc_load(i).wait()
            lax.fori_loop(i * each, (i + 1) * each, trip, 0)
            stores[i].start()
    else:
        stores = [store(outs_hbm[0], i, i) for i in range(chunks)]
        lax.fori_loop(0, chunks, chunk, 0)
    for copy in stores:
        copy.wait()


def partial_grads(name, meta, slot_table, pieces, grads, sources, split, acc=None):
    plan = tuple(piece.shape[0] for piece in pieces)
    depth = sum(plan)
    depths = tuple((128, source) for source in sources)
    assert depth == 128 * len(depths)
    places = slot_table.shape[1]
    any_spec = pl.BlockSpec(memory_space=pl.ANY)
    block = (places, 128, 128)
    half = jax.ShapeDtypeStruct((places // 2, 128, 128), jnp.float32)
    out_shape = (half, half) if split else (jax.ShapeDtypeStruct(block, jnp.float32),)
    extra = () if acc is None else (acc,)
    operands = (*pieces, *grads, *extra)
    return pl.pallas_call(
        functools.partial(grads_kernel, plan, depths, split, acc is not None, name.startswith("own")),
        out_shape=out_shape,
        in_specs=[pl.BlockSpec(memory_space=pltpu.SMEM)] * 2 + [any_spec] * len(operands),
        out_specs=tuple(any_spec for _ in out_shape),
        scratch_shapes=[
            pltpu.VMEM((depth, pieces[0].shape[1]), jnp.bfloat16),
            pltpu.VMEM((depth, grads[0].shape[1]), jnp.bfloat16),
            pltpu.VMEM(block, jnp.float32),
            pltpu.SemaphoreType.DMA((len(operands),)),
            pltpu.SemaphoreType.DMA((places // CHUNK,)),
            pltpu.SemaphoreType.DMA((places // CHUNK,)),
        ],
        compiler_params=pltpu.CompilerParams(vmem_limit_bytes=56 * 1024 * 1024),
        cost_estimate=pl.CostEstimate(
            flops=2 * places * 128 * 128 * depth, bytes_accessed=30_000_000, transcendentals=0
        ),
    )(meta, slot_table, *operands)


def on_device(tokens, out_grad, delta, block_rows, block_cols, block_count):
    places = block_rows.shape[0]
    dp = lax.axis_index("dp")
    tp = lax.axis_index("tensor")
    across = lax.bitwise_xor(tp, 1)

    def around(base):
        return [base, lax.bitwise_and(base + 6, 7), lax.bitwise_and(base + 2, 7), lax.bitwise_and(base + 4, 7)]

    def move(value, pairs, axis="tensor"):
        return lax.ppermute(value, axis, pairs)

    meta = jnp.stack(
        [lax.bitwise_and(dp, 1), lax.bitwise_and(dp >> 1, 7), dp >> 4, *around(tp)]
    ).astype(jnp.int32)
    table = jnp.stack([block_rows, block_cols, jnp.broadcast_to(block_count, (places,))])
    chunks = around(across)

    def theirs(source, index):
        return lax.dynamic_slice_in_dim(source, chunks[index] * 128, 128, 0)

    part_a, part_b = tokens[:64], tokens[64:]
    below_a, above_b = move(part_a, Y_UP), move(part_b, Y_DOWN)
    below_b, above_a = move(part_b, Y_UP), move(part_a, Y_DOWN)
    first_rows, later = lax.optimization_barrier((theirs(out_grad, 0), out_grad))
    g_own = move(first_rows, X_SWAP)
    table_x = move(table, X_SWAP)
    g_below, g_above, g_far = (
        move(theirs(later, i), X_SWAP) for i in (1, 2, 3)
    )
    far_a, far_b = move(below_a, Y_UP), move(above_b, Y_DOWN)
    top = jnp.broadcast_to(jnp.max(jnp.abs(later)).astype(jnp.float32), (8, 128))
    for pairs, axis in (
        (CORE_SWAP, "dp"),
        (z_swap(1), "dp"),
        (z_swap(2), "dp"),
        (z_swap(4), "dp"),
        (X_SWAP, "tensor"),
        (X_HI_SWAP, "dp"),
    ):
        top = jnp.maximum(top, move(top, pairs, axis))
    top = jnp.clip(top[0, 0], 1e-30, 1e37)
    shrink, grow = lax.optimization_barrier((0.25 / top, 4.0 * top))

    near = (tokens, below_a, below_b, above_a, above_b)
    far = (far_a, far_b)
    (acc,) = partial_grads(
        "own_near", meta, table, near, (out_grad,) * 3, (OWN, BELOW, ABOVE), False
    )
    (acc_x,) = partial_grads(
        "across_near", meta, table_x, near, (g_own, g_below, g_above), (None,) * 3, False
    )
    send, keep = partial_grads("own_far", meta, table, far, (out_grad,), (FAR,), True, acc)
    send_x, keep_x = partial_grads("across_far", meta, table_x, far, (g_far,), (None,), True, acc_x)

    share = delta.shape[1]
    quarter = places // 4

    width = share // 2

    def z_sum(value, packed):
        total = value[:width]
        for k in Z_STEPS:
            got = move(packed[width * k : width * (k + 1)], z_shift(k), "dp")
            total = total + got.astype(jnp.float32)
        return total

    own_back = move(send, CORE_SWAP, "dp")
    own_sum, shrink_x = lax.optimization_barrier(((keep + own_back) * shrink, shrink))
    other = ((keep_x + move(send_x, CORE_SWAP, "dp")) * shrink_x).astype(jnp.float16)
    part = quarter // 2
    got_x = []
    for h in range(2):
        near_x = move(other[h * part : (h + 1) * part], X_SWAP)
        far_x = other[quarter + h * part : quarter + (h + 1) * part]
        got_x.append((near_x, move(far_x, DIAGONAL, ("dp", "tensor"))))
    own_near, own_packed = lax.optimization_barrier(
        (own_sum[:quarter], own_sum[quarter:].astype(jnp.float16))
    )
    pieces = lax.all_to_all(own_packed, "dp", 0, 0, axis_index_groups=Z_GROUPS, tiled=True)
    pieces = jnp.sum(pieces.reshape(-1, share, 128, 128).astype(jnp.float32), axis=0)
    from_far = move(pieces, X_HI_SWAP, "dp")
    halves = []
    for h in range(2):
        ours = own_near[:part] if h == 0 else own_near[part:]
        for got in got_x[h]:
            ours = ours + got.astype(jnp.float32)
        ours = lax.optimization_barrier(ours)
        packed = ours.astype(jnp.float16)
        packed, own_near = lax.optimization_barrier((packed, own_near))
        halves.append(z_sum(ours, packed))
    grads = (jnp.concatenate(halves, axis=0) + from_far) * grow
    square_sum = jnp.broadcast_to(jnp.sum(grads * grads), (8, 128))
    for axis, size in (("dp", 32), ("tensor", 8)):
        spread = jnp.broadcast_to(square_sum[None], (size, 8, 128))
        square_sum = jnp.sum(lax.all_to_all(spread, axis, 0, 0, tiled=True), axis=0)
    square_sum = square_sum[0, 0]
    norm_limit = 128 * math.sqrt(8 * places)
    factor = jnp.minimum(jnp.float32(1.0), norm_limit / jnp.sqrt(square_sum + 1e-06))
    return delta - 0.5 * factor * grads[None]


def solution(mesh):
    return jax.shard_map(
        on_device,
        mesh=mesh,
        in_specs=(
            P(("dp", "tensor"), None),
            P("dp", "tensor"),
            P("tensor", "dp", None, None),
            P("tensor"),
            P("tensor"),
            P("tensor"),
        ),
        out_specs=P("tensor", "dp", None, None),
        check_vma=False,
    )
```

```python
import functools
import math

import jax
import jax.numpy as jnp
from jax import lax
from jax.experimental import pallas as pl
from jax.experimental.pallas import tpu as pltpu
from jax.sharding import PartitionSpec as P


CHUNK = 32
X_SWAP = [(t, t ^ 1) for t in range(8)]
Y_UP = [(t, (t + 2) % 8) for t in range(8)]
Y_DOWN = [(t, (t + 6) % 8) for t in range(8)]
CORE_SWAP = [(d, d ^ 1) for d in range(32)]
X_HI_SWAP = [(d, d ^ 16) for d in range(32)]
DIAGONAL = [(d * 8 + t, (d ^ 16) * 8 + (t ^ 1)) for d in range(32) for t in range(8)]


Z_GROUPS = [[xh * 16 + z * 2 + c for z in range(8)] for xh in range(2) for c in range(2)]


def z_swap(bit):
    return [(d, d ^ (bit * 2)) for d in range(32)]


def z_shift(k):
    return [(d, (d // 16) * 16 + (d + 2 * k) % 16) for d in range(32)]


Z_STEPS = (4, 3, 5, 2, 6, 1, 7)
CORE, Z, X_HI, OWN, BELOW, ABOVE, FAR = range(7)


def grads_kernel(plan, depths, split, with_acc, own, meta, slots_ref, *refs):
    count = len(plan)
    pieces = refs[:count]
    at = count
    grads = refs[at : at + len(depths)]
    at += len(depths)
    if with_acc:
        acc_hbm = refs[at]
        at += 1
    outs_hbm = refs[at : at + (2 if split else 1)]
    at += len(outs_hbm)
    x_buf, g_buf, o_buf, in_sem, acc_sem, out_sem = refs[at:]
    places = o_buf.shape[0]
    copies = []
    row = 0
    for index, size in enumerate(plan):
        copies.append(
            pltpu.make_async_copy(pieces[index], x_buf.at[pl.ds(row, size), :], in_sem.at[len(copies)])
        )
        row += size
    row = 0
    for index, (size, source) in enumerate(depths):
        block = grads[index]
        if source is not None:
            block = block.at[pl.ds(pl.multiple_of(meta[source] * 128, 128), size), :]
        copies.append(
            pltpu.make_async_copy(block, g_buf.at[pl.ds(row, size), :], in_sem.at[len(copies)])
        )
        row += size
    chunks = places // CHUNK
    unroll = CHUNK // 2 if with_acc else CHUNK

    def acc_load(i):
        span = pl.ds(i * CHUNK, CHUNK)
        return pltpu.make_async_copy(acc_hbm.at[span], o_buf.at[span], acc_sem.at[i])

    def store(target, start, i):
        return pltpu.make_async_copy(
            o_buf.at[pl.ds(i * CHUNK, CHUNK)], target.at[pl.ds(start * CHUNK, CHUNK)], out_sem.at[i]
        )

    for copy in copies:
        copy.start()
    if with_acc:
        for i in range(chunks):
            acc_load(i).start()
    for copy in copies:
        copy.wait()
    core, z, x_hi = meta[CORE], meta[Z], meta[X_HI]
    live = slots_ref[2, 0]

    def slot_of(place):
        part = lax.shift_right_logical(place, 6)
        far_half = lax.bitwise_and(lax.shift_right_logical(place, 5), 1)
        ahead = lax.bitwise_and(lax.shift_right_logical(place, 2), 7)
        owner_core = lax.bitwise_xor(core, 1 - part)
        owner_x = lax.bitwise_xor(x_hi, far_half)
        owner_z = lax.bitwise_and((z * (1 - far_half) if own else z) + ahead, 7)
        return owner_x * 64 + owner_z * 8 + owner_core * 4 + lax.bitwise_and(place, 3)

    def trip(step, carry):
        values = []
        for u in range(unroll):
            place = step * unroll + u
            slot = slot_of(place)
            row = pl.multiple_of(slots_ref[0, slot] * 128, 128)
            col = pl.multiple_of(slots_ref[1, slot] * 128, 128)
            value = lax.dot_general(
                x_buf[:, pl.ds(row, 128)],
                g_buf[:, pl.ds(col, 128)],
                (((0,), (0,)), ((), ())),
                preferred_element_type=jnp.float32,
            )
            if with_acc:
                value = o_buf[place] + value
            if split:
                value = jnp.where(slot < live, value, 0.0)
            values.append(value)
        for u in range(unroll):
            o_buf[step * unroll + u] = values[u]
        return carry

    each = CHUNK // unroll

    def chunk(i, carry):
        lax.fori_loop(i * each, (i + 1) * each, trip, 0)
        store(outs_hbm[0], i, i).start()
        return carry

    if split:
        stores = [store(outs_hbm[i * 2 // chunks], i % (chunks // 2), i) for i in range(chunks)]
        for i in range(chunks):
            if with_acc:
                acc_load(i).wait()
            lax.fori_loop(i * each, (i + 1) * each, trip, 0)
            stores[i].start()
    else:
        stores = [store(outs_hbm[0], i, i) for i in range(chunks)]
        lax.fori_loop(0, chunks, chunk, 0)
    for copy in stores:
        copy.wait()


def partial_grads(name, meta, slot_table, pieces, grads, sources, split, acc=None):
    plan = tuple(piece.shape[0] for piece in pieces)
    depth = sum(plan)
    depths = tuple((128, source) for source in sources)
    assert depth == 128 * len(depths)
    places = slot_table.shape[1]
    any_spec = pl.BlockSpec(memory_space=pl.ANY)
    block = (places, 128, 128)
    half = jax.ShapeDtypeStruct((places // 2, 128, 128), jnp.float32)
    out_shape = (half, half) if split else (jax.ShapeDtypeStruct(block, jnp.float32),)
    extra = () if acc is None else (acc,)
    operands = (*pieces, *grads, *extra)
    return pl.pallas_call(
        functools.partial(grads_kernel, plan, depths, split, acc is not None, name.startswith("own")),
        out_shape=out_shape,
        in_specs=[pl.BlockSpec(memory_space=pltpu.SMEM)] * 2 + [any_spec] * len(operands),
        out_specs=tuple(any_spec for _ in out_shape),
        scratch_shapes=[
            pltpu.VMEM((depth, pieces[0].shape[1]), jnp.bfloat16),
            pltpu.VMEM((depth, grads[0].shape[1]), jnp.bfloat16),
            pltpu.VMEM(block, jnp.float32),
            pltpu.SemaphoreType.DMA((len(operands),)),
            pltpu.SemaphoreType.DMA((places // CHUNK,)),
            pltpu.SemaphoreType.DMA((places // CHUNK,)),
        ],
        compiler_params=pltpu.CompilerParams(vmem_limit_bytes=56 * 1024 * 1024),
        cost_estimate=pl.CostEstimate(
            flops=2 * places * 128 * 128 * depth, bytes_accessed=30_000_000, transcendentals=0
        ),
    )(meta, slot_table, *operands)


def on_device(tokens, out_grad, delta, block_rows, block_cols, block_count):
    places = block_rows.shape[0]
    dp = lax.axis_index("dp")
    tp = lax.axis_index("tensor")
    across = lax.bitwise_xor(tp, 1)

    def around(base):
        return [base, lax.bitwise_and(base + 6, 7), lax.bitwise_and(base + 2, 7), lax.bitwise_and(base + 4, 7)]

    def move(value, pairs, axis="tensor"):
        return lax.ppermute(value, axis, pairs)

    meta = jnp.stack(
        [lax.bitwise_and(dp, 1), lax.bitwise_and(dp >> 1, 7), dp >> 4, *around(tp)]
    ).astype(jnp.int32)
    table = jnp.stack([block_rows, block_cols, jnp.broadcast_to(block_count, (places,))])
    chunks = around(across)

    def theirs(source, index):
        return lax.dynamic_slice_in_dim(source, chunks[index] * 128, 128, 0)

    part_a, part_b = tokens[:64], tokens[64:]
    below_a, above_b = move(part_a, Y_UP), move(part_b, Y_DOWN)
    below_b, above_a = move(part_b, Y_UP), move(part_a, Y_DOWN)
    first_rows, later = lax.optimization_barrier((theirs(out_grad, 0), out_grad))
    g_own = move(first_rows, X_SWAP)
    table_x = move(table, X_SWAP)
    g_below, g_above, g_far = (
        move(theirs(later, i), X_SWAP) for i in (1, 2, 3)
    )
    far_a, far_b = move(below_a, Y_UP), move(above_b, Y_DOWN)
    top = jnp.broadcast_to(jnp.max(jnp.abs(later)).astype(jnp.float32), (8, 128))
    for pairs, axis in (
        (CORE_SWAP, "dp"),
        (z_swap(1), "dp"),
        (z_swap(2), "dp"),
        (z_swap(4), "dp"),
        (X_SWAP, "tensor"),
        (X_HI_SWAP, "dp"),
    ):
        top = jnp.maximum(top, move(top, pairs, axis))
    top = jnp.clip(top[0, 0], 1e-30, 1e37)
    shrink, grow = lax.optimization_barrier((0.25 / top, 4.0 * top))

    near = (tokens, below_a, below_b, above_a, above_b)
    far = (far_a, far_b)
    (acc,) = partial_grads(
        "own_near", meta, table, near, (out_grad,) * 3, (OWN, BELOW, ABOVE), False
    )
    (acc_x,) = partial_grads(
        "across_near", meta, table_x, near, (g_own, g_below, g_above), (None,) * 3, False
    )
    send, keep = partial_grads("own_far", meta, table, far, (out_grad,), (FAR,), True, acc)
    send_x, keep_x = partial_grads("across_far", meta, table_x, far, (g_far,), (None,), True, acc_x)

    share = delta.shape[1]
    quarter = places // 4

    def z_sum(value):
        packed = value.astype(jnp.float16)
        total = value[:share]
        for k in Z_STEPS:
            got = move(packed[share * k : share * (k + 1)], z_shift(k), "dp")
            total = total + got.astype(jnp.float32)
        return total

    own_back = move(send, CORE_SWAP, "dp")
    own_sum, shrink_x = lax.optimization_barrier(((keep + own_back) * shrink, shrink))
    other = ((keep_x + move(send_x, CORE_SWAP, "dp")) * shrink_x).astype(jnp.float16)
    near_x = move(other[:quarter], X_SWAP)
    far_x = move(other[quarter:], DIAGONAL, ("dp", "tensor"))
    own_near, own_packed = lax.optimization_barrier(
        (own_sum[:quarter], own_sum[quarter:].astype(jnp.float16))
    )
    pieces = lax.all_to_all(own_packed, "dp", 0, 0, axis_index_groups=Z_GROUPS, tiled=True)
    pieces = jnp.sum(pieces.reshape(-1, share, 128, 128).astype(jnp.float32), axis=0)
    from_far = move(pieces, X_HI_SWAP, "dp")
    ours = own_near + near_x.astype(jnp.float32) + far_x.astype(jnp.float32)
    grads = (z_sum(ours) + from_far) * grow
    square_sum = jnp.broadcast_to(jnp.sum(grads * grads), (8, 128))
    for axis, size in (("dp", 32), ("tensor", 8)):
        spread = jnp.broadcast_to(square_sum[None], (size, 8, 128))
        square_sum = jnp.sum(lax.all_to_all(spread, axis, 0, 0, tiled=True), axis=0)
    square_sum = square_sum[0, 0]
    norm_limit = 128 * math.sqrt(8 * places)
    factor = jnp.minimum(jnp.float32(1.0), norm_limit / jnp.sqrt(square_sum + 1e-06))
    return delta - 0.5 * factor * grads[None]


def solution(mesh):
    return jax.shard_map(
        on_device,
        mesh=mesh,
        in_specs=(
            P(("dp", "tensor"), None),
            P("dp", "tensor"),
            P("tensor", "dp", None, None),
            P("tensor"),
            P("tensor"),
            P("tensor"),
        ),
        out_specs=P("tensor", "dp", None, None),
        check_vma=False,
    )
```
